32 devices in a mesh: sa: 8 (over z, y), sb: 4 (over x, core).
Axes of the slice: x: 2, y: 2, z: 4, core: 2. Of those that a mesh axis runs over, the one named last changes fastest.
Arguments:
- queries: bfloat16 [16384, 4096], P(('sa', 'sb')), may hold values from -6 to 6
- keys: bfloat16 [16384, 4096], P(('sa', 'sb')), may hold values from -0.5390625 to 0.5390625
- values: bfloat16 [16384, 2048], P(('sa', 'sb')), may hold values from -6 to 6
- level_weights: bfloat16 [16384, 15, 32], P(('sa', 'sb')), may hold values from 0.25 to 4
- out_gain: bfloat16 [2048], replicated, may hold values from 0.25 to 1.75
Outputs:
- mixed: bfloat16 [16384, 2048], P(('sa', 'sb'))
The draws below stay inside these ranges and needn't reach their ends.
All inputs are finite; a program needn't handle non-finite values.
Results may differ from the reference program's by a relative error of at most 0.008.
Values sent between devices are 32-bit elements; how exact they have to be, the bound alone decides.
A program may use at most 192 MiB of HBM per device.

```python
import math
import jax
import jax.numpy as jnp
from jax import lax

H = 32
DK = 128
DV = 64
TOK_DEV = 512
TOK_BITS = 9
DEV_BITS = 5
LEVELS = 15
TOKENS = 16384
N_SA = 8
N_SB = 4


def block_scale(own_key, shape, split, smallest, top_value):
    gain, own = 1.0, jax.random.fold_in(own_key, 6)
    for dim, parts in split:
        draws = jnp.exp(jax.random.uniform(jax.random.fold_in(own, dim), (parts,), jnp.float32, smallest / len(split), top_value / len(split)))
        gain = gain * jnp.repeat(draws, shape[dim] // parts).reshape([-1 if axis == dim else 1 for axis in range(len(shape))])
    return gain


def normal_values(own_key, shape, width, limit, cuts=(), held_as=jnp.bfloat16):
    values = jax.random.normal(own_key, shape, jnp.float32) * width
    if len(cuts) > 0:
        values = block_scale(own_key, shape, cuts, -0.22, 0.18) * values
    return jnp.clip(values, min=-limit, max=limit).astype(held_as)


def setup_inputs(seed: int = 0) -> dict:
    streams_of = jax.random.split(jax.random.key(seed), 6)
    return {
        "queries": normal_values(streams_of[0], (TOKENS, H * DK), 1.0, 6.0, ((0, 32),)),
        "keys": normal_values(streams_of[1], (TOKENS, H * DK), 0.09, 0.5390625, ((0, 32),)),
        "values": normal_values(streams_of[2], (TOKENS, H * DV), 1.0, 6.0, ((0, 32),)),
        "level_weights": jnp.clip(jnp.exp(math.log(4.0) - 2.7725887 * jax.random.uniform(streams_of[3], (TOKENS, LEVELS, H), jnp.float32) ** block_scale(streams_of[3], (TOKENS, LEVELS, H), ((0, 32),), -0.2, 0.2)), 0.25, 4.0).astype(jnp.bfloat16),
        "out_gain": jnp.clip(1.0 + 0.15 * jax.random.normal(streams_of[4], (H * DV,), jnp.float32), 0.25, 1.75).astype(jnp.bfloat16),
    }


epsilon = 1e-06

def block_levels(length):
    position = jnp.arange(length, dtype=jnp.int32)
    xored = jnp.bitwise_xor(position[:, None], position[None, :])
    level_index = jnp.zeros((length, length), jnp.int32)
    for level_bit in range(TOK_BITS):
        level_index = level_index + (xored >= 1 << level_bit).astype(jnp.int32)
    level_table = level_index[:, :, None] == jnp.arange(TOK_BITS + 1, dtype=jnp.int32)[None, None, :]
    causal = position[:, None] >= position[None, :]
    return (level_table & causal[:, :, None]).astype(jnp.float32)

def local_block(level_table, query_matrix_rows, key_matrix_rows, value_matrix_rows, weight_rows):
    weight = jnp.einsum('tsl,tlh->hts', level_table, weight_rows[:, :TOK_BITS + 1, :].astype(jnp.float32), precision=lax.Precision.HIGHEST)
    scores = jnp.einsum('thk,shk->hts', query_matrix_rows.astype(jnp.float32), key_matrix_rows.astype(jnp.float32), precision=lax.Precision.HIGHEST)
    weighted = (scores * weight).astype(jnp.bfloat16)
    summed = jnp.einsum('hts,shv->thv', weighted.astype(jnp.float32), value_matrix_rows.astype(jnp.float32), precision=lax.Precision.HIGHEST)
    segment_block_state = jnp.einsum('tdw,tdr->dwr', key_matrix_rows.astype(jnp.float32), value_matrix_rows.astype(jnp.float32), precision=lax.Precision.HIGHEST)
    return (summed, segment_block_state)

def normalize(summed, out_gain):
    inverse_rms = lax.rsqrt(lax.optimization_barrier(jnp.mean(summed * summed, axis=-1, keepdims=True)) + epsilon)
    gain_rows = out_gain.reshape(H, DV).astype(jnp.float32)
    return (summed * inverse_rms * gain_rows).reshape(summed.shape[0], H * DV).astype(jnp.bfloat16)

def reference(queries, keys, values, level_weights, out_gain):
    blocks = N_SA * N_SB
    query_blocks = queries.reshape(blocks, TOK_DEV, H, DK)
    key_blocks = keys.reshape(blocks, TOK_DEV, H, DK)
    value_blocks = values.reshape(blocks, TOK_DEV, H, DV)
    weight_blocks = level_weights.reshape(blocks, TOK_DEV, LEVELS, H)
    level_table = block_levels(TOK_DEV)
    local_sums, states = lax.map(lambda pieces: local_block(level_table, *pieces), (query_blocks, key_blocks, value_blocks, weight_blocks))
    level_sums = []
    current = states
    for rank_bit in range(DEV_BITS):
        level_sums.append(current)
        current = current.reshape(-1, 2, H, DK, DV).sum(1)

    def finish(pieces):
        block_index, query_matrix_rows, weight_rows, summed = pieces
        query_single_float = query_matrix_rows.astype(jnp.float32)
        for rank_bit in range(DEV_BITS):
            partner = jnp.bitwise_xor(block_index >> rank_bit, 1).astype(jnp.int32)
            fenwick_level_state = lax.dynamic_index_in_dim(level_sums[rank_bit], partner, 0, keepdims=False)
            active_flag = (block_index >> rank_bit & 1).astype(jnp.float32)
            state_readout_output = jnp.einsum('jeu,eud->jed', query_single_float, fenwick_level_state, precision=lax.Precision.HIGHEST)
            factor = weight_rows[:, TOK_BITS + 1 + rank_bit, :].astype(jnp.float32) * active_flag
            summed = summed + factor[:, :, None] * state_readout_output
        return normalize(summed, out_gain)
    block_ids = jnp.arange(blocks, dtype=jnp.int32)
    mixed = lax.map(finish, (block_ids, query_blocks, weight_blocks, local_sums))
    return mixed.reshape(TOKENS, H * DV)
```

```python
import functools

import jax
import jax.numpy as jnp
from jax import lax
from jax.experimental import pallas as pl
from jax.experimental.pallas import tpu as pltpu
from jax.sharding import PartitionSpec as P

DK = 128
DV = 64
TOK_BITS = 9
LANES = 128
TILE_BITS = 7
ROWS = 256
OWNED = 1

epsilon = 1e-06
MESH = pl.DeviceIdType.MESH
NT = (((1,), (1,)), ((), ()))
TN = (((0,), (0,)), ((), ()))


def lane_gather(value, index):
    return jnp.take_along_axis(value, index, axis=1, mode="promise_in_bounds")


def kernel(
    inner_bits, levels, chunks, slots, zero_slot,
    q_hbm, k_hbm, v_hbm, w_hbm, gain_ref, out_hbm,
    qb, kb, vb, wb, acc, ob, st, lvl, car, table,
    in_sem, out_sem, send_sem, recv_sem, pass_send, pass_recv,
):
    inner, outer = lax.axis_index("sb"), lax.axis_index("sa")
    length = qb.shape[1]
    pairs = 2 * OWNED
    core = inner % 2

    def bit(j):
        if j < inner_bits:
            return (inner // (1 << j)) % 2
        return (outer // (1 << (j - inner_bits))) % 2

    def partner(j):
        if j < inner_bits:
            return {"sb": inner + (1 << j) * (1 - 2 * bit(j))}
        return {"sa": outer + (1 << (j - inner_bits)) * (1 - 2 * bit(j))}

    def fetch(which, c):
        source, target, width = (
            (k_hbm, kb, 2 * pairs * DK), (v_hbm, vb, 2 * pairs * DV), (q_hbm, qb, 2 * pairs * DK)
        )[which]
        columns = pl.ds(pl.multiple_of(c * width, width), width)
        return pltpu.make_async_copy(source.at[:, columns], target.at[c], in_sem.at[which, c])

    weights_copy = pltpu.make_async_copy(w_hbm, wb, in_sem.at[3, 0])

    def put(c):
        width = pairs * 2 * DV
        columns = pl.ds(pl.multiple_of(c * width, width), width)
        return pltpu.make_async_copy(ob.at[c], out_hbm.at[:, columns], out_sem.at[c])

    mine = pl.ds(core * OWNED, OWNED)

    def exchange(j, c):
        if j == 0:
            source, target = st.at[c], lvl.at[0, c]
        else:
            source, target = car.at[j - 1, c], lvl.at[j, c, mine]
        return pltpu.make_async_remote_copy(
            src_ref=source, dst_ref=target, send_sem=send_sem.at[j, c],
            recv_sem=recv_sem.at[j, c], device_id=partner(j), device_id_type=MESH,
        )

    def pass_on(j, c):
        return pltpu.make_async_remote_copy(
            src_ref=lvl.at[j, c, mine], dst_ref=lvl.at[j, c, mine], send_sem=pass_send.at[j, c],
            recv_sem=pass_recv.at[j, c], device_id=partner(0), device_id_type=MESH,
        )

    for c in range(chunks):
        fetch(0, c).start()
        fetch(1, c).start()
        if c == 0:
            weights_copy.start()
            fetch(2, 0).start()
    for c in range(1, chunks):
        fetch(2, c).start()

    barrier = pltpu.get_barrier_semaphore()
    for j in range(levels):
        pl.semaphore_signal(barrier, inc=1, device_id=partner(j), device_id_type=MESH)

    row = lax.broadcasted_iota(jnp.int32, (LANES, LANES), 0)
    lane = lax.broadcasted_iota(jnp.int32, (LANES, LANES), 1)
    xored = jnp.bitwise_xor(row, lane)
    level = jnp.zeros((LANES, LANES), jnp.int32)
    for b in range(TILE_BITS):
        level = level + (xored >= (1 << b)).astype(jnp.int32)
    table[...] = jnp.where(row >= lane, level, zero_slot)
    pl.semaphore_wait(barrier, levels)

    def weight_place(c):
        start = c * (2 * pairs * slots)
        return start // LANES, start % LANES

    def block_states(c):
        for p in range(pairs):
            v = vb[c, :, p * 2 * DV : (p + 1) * 2 * DV]
            k = kb[c, :, p * 2 * DK : (p + 1) * 2 * DK]
            both = lax.dot_general(v, k, TN, preferred_element_type=jnp.float32)
            st[c, p, :DV, :] = both[:DV, :DK]
            st[c, p, DV:, :] = both[DV:, DK:]

    def local(c):
        group, offset = weight_place(c)
        for p in range(pairs):
            v = vb[c, :, p * 2 * DV : (p + 1) * 2 * DV]
            first = lax.broadcasted_iota(jnp.int32, v.shape, 1) < DV
            sides = (jnp.where(first, v, jnp.zeros_like(v)), jnp.where(first, jnp.zeros_like(v), v))
            for start in range(0, length, ROWS):
                total = None
                end = start + ROWS
                for side in range(2):
                    head = 2 * p + side
                    base = offset + head * slots
                    columns = slice(head * DK, (head + 1) * DK)
                    scores = lax.dot_general(
                        qb[c, start:end, columns], kb[c, :end, columns], NT,
                        preferred_element_type=jnp.float32,
                    )
                    strips = []
                    for t in range(start, end, LANES):
                        rows = wb[group, t : t + LANES, :]
                        strip, known = [], {}
                        for s in range(0, end, LANES):
                            if s > t:
                                strip.append(jnp.zeros((LANES, LANES), jnp.bfloat16))
                                continue
                            if s == t:
                                weight = lane_gather(rows, table[...] + base)
                            else:
                                number = (t ^ s).bit_length()
                                if number not in known:
                                    known[number] = lane_gather(
                                        rows, jnp.zeros((LANES, LANES), jnp.int32) + (base + number)
                                    )
                                weight = known[number]
                            piece = scores[t - start : t - start + LANES, s : s + LANES]
                            strip.append((piece * weight).astype(jnp.bfloat16))
                        strips.append(jnp.concatenate(strip, axis=1))
                    weighted = jnp.concatenate(strips, axis=0)
                    part = jnp.dot(weighted, sides[side][:end], preferred_element_type=jnp.float32)
                    total = part if total is None else total + part
                acc[c, start:end, p * LANES : (p + 1) * LANES] = total

    def finish(c):
        group, offset = weight_place(c)
        for p in range(pairs):
            states = []
            zero = jnp.zeros((DV, DK), jnp.bfloat16)
            for j in range(levels):
                state = jnp.where(bit(j) == 1, lvl[j, c, p], 0.0).astype(jnp.bfloat16)
                states.append(jnp.concatenate([state[:DV], zero], axis=1))
                states.append(jnp.concatenate([zero, state[DV:]], axis=1))
            for start in range(0, length, ROWS):
                q = qb[c, start : start + ROWS, p * 2 * DK : (p + 1) * 2 * DK]
                rows = wb[group, start : start + ROWS, :]
                right = (lax.broadcasted_iota(jnp.int32, (ROWS, LANES), 1) >= DV).astype(jnp.int32)
                place = right * slots + (offset + 2 * p * slots + TOK_BITS + 1)
                total = acc[c, start : start + ROWS, p * LANES : (p + 1) * LANES]
                for j in range(0, levels, 2):
                    stacked = jnp.concatenate(states[2 * j : 2 * j + 4], axis=0)
                    read = lax.dot_general(q, stacked, NT, preferred_element_type=jnp.float32)
                    for i in range(j, min(j + 2, levels)):
                        total = total + lane_gather(rows, place + i) * read[:, (i - j) * LANES : (i - j + 1) * LANES]
                square = total * total
                left = jnp.sum(jnp.where(right == 0, square, 0.0), axis=1, keepdims=True)
                other = jnp.sum(jnp.where(right == 0, 0.0, square), axis=1, keepdims=True)
                scale = jnp.where(
                    right == 0, lax.rsqrt(left * (1.0 / DV) + epsilon), lax.rsqrt(other * (1.0 / DV) + epsilon)
                )
                gain = gain_ref[c, :, p * LANES : (p + 1) * LANES]
                ob[c, start : start + ROWS, p * LANES : (p + 1) * LANES] = (total * scale * gain).astype(jnp.bfloat16)

    @pl.loop(0, chunks + levels + 1)
    def _(tick):
        @pl.when(tick < chunks)
        def _():
            fetch(0, tick).wait()
            fetch(1, tick).wait()
            block_states(tick)
            exchange(0, tick).start()

        for j in range(levels):
            c = tick - 1 - j

            @pl.when((c >= 0) & (c < chunks))
            def _(j=j, c=c):
                exchange(j, c).wait_recv()
                if j > 0:
                    pass_on(j, c).start()
                if j + 1 < levels:
                    own = st[c, mine] if j == 0 else car[j - 1, c]
                    car[j, c] = own + lvl[j, c, mine]
                    exchange(j + 1, c).start()

        @pl.when(tick == 0)
        def _():
            weights_copy.wait()

        @pl.when(tick < chunks)
        def _():
            fetch(2, tick).wait()
            local(tick)

        @pl.when(tick >= levels + 1)
        def _():
            c = tick - levels - 1
            for j in range(1, levels):
                pass_on(j, c).wait_recv()
            finish(c)
            put(c).start()

    @pl.loop(0, chunks)
    def _(c):
        put(c).wait()
        for j in range(levels):
            exchange(j, c).wait_send()
            if j > 0:
                pass_on(j, c).wait_send()


def on_device(queries, keys, values, level_weights, out_gain):
    length = queries.shape[0]
    heads = out_gain.shape[0] // DV
    count = level_weights.shape[1]
    inner_bits = lax.axis_size("sb").bit_length() - 1
    levels = inner_bits + lax.axis_size("sa").bit_length() - 1
    slots = 1 << count.bit_length()
    pairs = 2 * OWNED
    chunks = heads // (2 * pairs)
    weights = jnp.transpose(level_weights, (0, 2, 1))
    weights = jnp.pad(weights, ((0, 0), (0, 0), (0, slots - count)))
    weights = weights.reshape(length, heads * slots // LANES, LANES).astype(jnp.float32)
    weights = jnp.transpose(weights, (1, 0, 2))
    gain = out_gain.reshape(chunks, 1, pairs * 2 * DV).astype(jnp.float32)
    hbm = pl.BlockSpec(memory_space=pl.ANY)
    dma = pltpu.SemaphoreType.DMA
    return pl.pallas_call(
        functools.partial(kernel, inner_bits, levels, chunks, slots, count),
        out_shape=jax.ShapeDtypeStruct(values.shape, jnp.bfloat16),
        in_specs=[hbm, hbm, hbm, hbm, pl.BlockSpec(memory_space=pltpu.VMEM)],
        out_specs=hbm,
        scratch_shapes=[
            pltpu.VMEM((chunks, length, 2 * pairs * DK), jnp.bfloat16),
            pltpu.VMEM((chunks, length, 2 * pairs * DK), jnp.bfloat16),
            pltpu.VMEM((chunks, length, 2 * pairs * DV), jnp.bfloat16),
            pltpu.VMEM(weights.shape, jnp.float32),
            pltpu.VMEM((chunks, length, 2 * pairs * DV), jnp.float32),
            pltpu.VMEM((chunks, length, 2 * pairs * DV), jnp.bfloat16),
            pltpu.VMEM((chunks, pairs, 2 * DV, DK), jnp.float32),
            pltpu.VMEM((levels, chunks, pairs, 2 * DV, DK), jnp.float32),
            pltpu.VMEM((levels - 1, chunks, OWNED, 2 * DV, DK), jnp.float32),
            pltpu.VMEM((LANES, LANES), jnp.int32),
            dma((4, chunks)),
            dma((chunks,)),
            dma((levels, chunks)),
            dma((levels, chunks)),
            dma((levels, chunks)),
            dma((levels, chunks)),
        ],
        compiler_params=pltpu.CompilerParams(
            collective_id=0, has_side_effects=True, vmem_limit_bytes=56 * 1024 * 1024
        ),
    )(queries, keys, values, weights, gain)


def solution(mesh):
    return jax.shard_map(
        on_device,
        mesh=mesh,
        in_specs=(
            P(("sa", "sb"), None),
            P(("sa", "sb"), None),
            P(("sa", "sb"), None),
            P(("sa", "sb"), None, None),
            P(),
        ),
        out_specs=P(("sa", "sb"), None),
        check_vma=False,
    )
```

```python
import functools

import jax
import jax.numpy as jnp
from jax import lax
from jax.experimental import pallas as pl
from jax.experimental.pallas import tpu as pltpu
from jax.sharding import PartitionSpec as P

DK = 128
DV = 64
TOK_BITS = 9
LANES = 128
TILE_BITS = 7
ROWS = 256
OWNED = 1
NEAR = 3
VMEM_MIB = 56
NEAR_GAP = 2
FAR_GAP = 2

epsilon = 1e-06
MESH = pl.DeviceIdType.MESH
NT = (((1,), (1,)), ((), ()))
TN = (((0,), (0,)), ((), ()))


def lane_gather(value, index):
    return jnp.take_along_axis(value, index, axis=1, mode="promise_in_bounds")


def kernel(
    inner_bits, levels, chunks, slots, zero_slot, heads,
    q_hbm, k_hbm, v_hbm, w_hbm, out_hbm,
    qb, kb, vb, wt, wb, acc, ob, st, lvl, car, table,
    in_sem, out_sem, send_sem, recv_sem, pass_send, pass_recv,
):
    inner, outer = lax.axis_index("sb"), lax.axis_index("sa")
    length = qb.shape[1]
    pairs = 2 * OWNED
    core = inner % 2

    def bit(j):
        if j < inner_bits:
            return (inner // (1 << j)) % 2
        return (outer // (1 << (j - inner_bits))) % 2

    def partner(j):
        if j < inner_bits:
            return {"sb": inner + (1 << j) * (1 - 2 * bit(j))}
        return {"sa": outer + (1 << (j - inner_bits)) * (1 - 2 * bit(j))}

    def fetch(which, c):
        source, target, width = (
            (k_hbm, kb, 2 * pairs * DK), (v_hbm, vb, 2 * pairs * DV), (q_hbm, qb, 2 * pairs * DK)
        )[which]
        columns = pl.ds(pl.multiple_of(c * width, width), width)
        return pltpu.make_async_copy(source.at[:, columns], target.at[c], in_sem.at[which, c])

    weights_copy = pltpu.make_async_copy(w_hbm, wt, in_sem.at[3, 0])

    def put(c):
        width = pairs * 2 * DV
        columns = pl.ds(pl.multiple_of(c * width, width), width)
        return pltpu.make_async_copy(ob.at[c], out_hbm.at[:, columns], out_sem.at[c])

    mine = pl.ds(core * OWNED, OWNED)

    def exchange(j, c):
        if j == 0:
            source, target = st.at[c], lvl.at[0, c]
        else:
            source, target = car.at[j - 1, c], lvl.at[j, c, mine]
        return pltpu.make_async_remote_copy(
            src_ref=source, dst_ref=target, send_sem=send_sem.at[j, c],
            recv_sem=recv_sem.at[j, c], device_id=partner(j), device_id_type=MESH,
        )

    def pass_on(j, c):
        return pltpu.make_async_remote_copy(
            src_ref=lvl.at[j, c, mine], dst_ref=lvl.at[j, c, mine], send_sem=pass_send.at[j, c],
            recv_sem=pass_recv.at[j, c], device_id=partner(0), device_id_type=MESH,
        )

    for c in range(chunks):
        fetch(0, c).start()
        fetch(1, c).start()
        if c == 0:
            weights_copy.start()
            fetch(2, 0).start()
    for c in range(1, chunks):
        fetch(2, c).start()

    barrier = pltpu.get_barrier_semaphore()
    for j in range(levels):
        pl.semaphore_signal(barrier, inc=1, device_id=partner(j), device_id_type=MESH)

    row = lax.broadcasted_iota(jnp.int32, (LANES, LANES), 0)
    lane = lax.broadcasted_iota(jnp.int32, (LANES, LANES), 1)
    xored = jnp.bitwise_xor(row, lane)
    level = jnp.zeros((LANES, LANES), jnp.int32)
    for b in range(TILE_BITS):
        level = level + (xored >= (1 << b)).astype(jnp.int32)
    table[...] = jnp.where(row >= lane, level, zero_slot)
    pl.semaphore_wait(barrier, levels)

    def weight_place(c):
        start = c * (2 * pairs * slots)
        return start // LANES, start % LANES

    def spread_weights(group):
        shape = (wt.shape[0], LANES)
        slot = lax.broadcasted_iota(jnp.int32, shape, 1) + group * LANES
        wanted = (slot & (slots - 1)) * heads + lax.shift_right_logical(slot, slots.bit_length() - 1)
        chosen = (lax.broadcasted_iota(jnp.int32, shape, 0) == wanted).astype(jnp.bfloat16)
        wb[group] = lax.dot_general(wt[...], chosen, TN, preferred_element_type=jnp.float32)

    def block_states(c):
        for p in range(pairs):
            v = vb[c, :, p * 2 * DV : (p + 1) * 2 * DV]
            k = kb[c, :, p * 2 * DK : (p + 1) * 2 * DK]
            both = lax.dot_general(v, k, TN, preferred_element_type=jnp.float32)
            st[c, p, :DV, :] = both[:DV, :DK]
            st[c, p, DV:, :] = both[DV:, DK:]

    def local(c):
        group, offset = weight_place(c)
        for p in range(pairs):
            v = vb[c, :, p * 2 * DV : (p + 1) * 2 * DV]
            first = lax.broadcasted_iota(jnp.int32, v.shape, 1) < DV
            sides = (jnp.where(first, v, jnp.zeros_like(v)), jnp.where(first, jnp.zeros_like(v), v))
            for start in range(0, length, ROWS):
                total = None
                end = start + ROWS
                for side in range(2):
                    head = 2 * p + side
                    base = offset + head * slots
                    columns = slice(head * DK, (head + 1) * DK)
                    scores = lax.dot_general(
                        qb[c, start:end, columns], kb[c, :end, columns], NT,
                        preferred_element_type=jnp.float32,
                    )
                    strips = []
                    for t in range(start, end, LANES):
                        rows = wb[group, t : t + LANES, :]
                        strip, known = [], {}
                        for s in range(0, end, LANES):
                            if s > t:
                                strip.append(jnp.zeros((LANES, LANES), jnp.bfloat16))
                                continue
                            if s == t:
                                weight = lane_gather(rows, table[...] + base)
                            else:
                                number = (t ^ s).bit_length()
                                if number not in known:
                                    known[number] = lane_gather(
                                        rows, jnp.zeros((LANES, LANES), jnp.int32) + (base + number)
                                    )
                                weight = known[number]
                            piece = scores[t - start : t - start + LANES, s : s + LANES]
                            strip.append((piece * weight).astype(jnp.bfloat16))
                        strips.append(jnp.concatenate(strip, axis=1))
                    weighted = jnp.concatenate(strips, axis=0)
                    part = jnp.dot(weighted, sides[side][:end], preferred_element_type=jnp.float32)
                    total = part if total is None else total + part
                acc[c, start:end, p * LANES : (p + 1) * LANES] = total

    def finish(c):
        group, offset = weight_place(c)
        for p in range(pairs):
            states = []
            zero = jnp.zeros((DV, DK), jnp.bfloat16)
            for j in range(levels):
                state = jnp.where(bit(j) == 1, lvl[j, c, p], 0.0).astype(jnp.bfloat16)
                states.append(jnp.concatenate([state[:DV], zero], axis=1))
                states.append(jnp.concatenate([zero, state[DV:]], axis=1))
            for start in range(0, length, ROWS):
                q = qb[c, start : start + ROWS, p * 2 * DK : (p + 1) * 2 * DK]
                rows = wb[group, start : start + ROWS, :]
                right = (lax.broadcasted_iota(jnp.int32, (ROWS, LANES), 1) >= DV).astype(jnp.int32)
                place = right * slots + (offset + 2 * p * slots + TOK_BITS + 1)
                total = acc[c, start : start + ROWS, p * LANES : (p + 1) * LANES]
                for j in range(0, levels, 2):
                    stacked = jnp.concatenate(states[2 * j : 2 * j + 4], axis=0)
                    read = lax.dot_general(q, stacked, NT, preferred_element_type=jnp.float32)
                    for i in range(j, min(j + 2, levels)):
                        total = total + lane_gather(rows, place + i) * read[:, (i - j) * LANES : (i - j + 1) * LANES]
                square = total * total
                left = jnp.sum(jnp.where(right == 0, square, 0.0), axis=1, keepdims=True)
                other = jnp.sum(jnp.where(right == 0, 0.0, square), axis=1, keepdims=True)
                scale = jnp.where(
                    right == 0, lax.rsqrt(left * (1.0 / DV) + epsilon), lax.rsqrt(other * (1.0 / DV) + epsilon)
                )
                ob[c, start : start + ROWS, p * LANES : (p + 1) * LANES] = (total * scale).astype(jnp.bfloat16)

    arrival = [1]
    for j in range(1, levels):
        arrival.append(arrival[-1] + (NEAR_GAP if j < NEAR else FAR_GAP))
    last = arrival[-1] + 1

    @pl.loop(0, chunks + last)
    def _(tick):
        @pl.when(tick < chunks)
        def _():
            fetch(0, tick).wait()
            fetch(1, tick).wait()
            block_states(tick)
            exchange(0, tick).start()

        for j in range(levels):
            c = tick - arrival[j]

            @pl.when((c >= 0) & (c < chunks))
            def _(j=j, c=c):
                exchange(j, c).wait_recv()
                if j > 0:
                    pass_on(j, c).start()
                if j + 1 < levels:
                    own = st[c, mine] if j == 0 else car[j - 1, c]
                    car[j, c] = own + lvl[j, c, mine]
                    exchange(j + 1, c).start()

        @pl.when(tick == 0)
        def _():
            weights_copy.wait()

        @pl.when(tick < chunks)
        def _():
            fetch(2, tick).wait()
            group, offset = weight_place(tick)

            @pl.when(offset == 0)
            def _():
                spread_weights(group)

            local(tick)

        @pl.when(tick >= last)
        def _():
            c = tick - last
            for j in range(1, levels):
                pass_on(j, c).wait_recv()
            finish(c)
            put(c).start()

    @pl.loop(0, chunks)
    def _(c):
        put(c).wait()
        for j in range(levels):
            exchange(j, c).wait_send()
            if j > 0:
                pass_on(j, c).wait_send()


def on_device(queries, keys, values, level_weights, out_gain):
    length = queries.shape[0]
    heads = out_gain.shape[0] // DV
    count = level_weights.shape[1]
    inner_bits = lax.axis_size("sb").bit_length() - 1
    levels = inner_bits + lax.axis_size("sa").bit_length() - 1
    slots = 1 << count.bit_length()
    pairs = 2 * OWNED
    chunks = heads // (2 * pairs)
    weights = jnp.transpose(level_weights, (1, 2, 0)).reshape(count * heads, length)
    hbm = pl.BlockSpec(memory_space=pltpu.HBM)
    dma = pltpu.SemaphoreType.DMA
    unit = pl.pallas_call(
        functools.partial(kernel, inner_bits, levels, chunks, slots, count, heads),
        out_shape=jax.ShapeDtypeStruct(values.shape, jnp.bfloat16),
        in_specs=[hbm, hbm, hbm, hbm],
        out_specs=pl.BlockSpec(memory_space=pl.ANY),
        scratch_shapes=[
            pltpu.VMEM((chunks, length, 2 * pairs * DK), jnp.bfloat16),
            pltpu.VMEM((chunks, length, 2 * pairs * DK), jnp.bfloat16),
            pltpu.VMEM((chunks, length, 2 * pairs * DV), jnp.bfloat16),
            pltpu.VMEM(weights.shape, jnp.bfloat16),
            pltpu.VMEM((heads * slots // LANES, length, LANES), jnp.float32),
            pltpu.VMEM((chunks, length, 2 * pairs * DV), jnp.float32),
            pltpu.VMEM((chunks, length, 2 * pairs * DV), jnp.bfloat16),
            pltpu.VMEM((chunks, pairs, 2 * DV, DK), jnp.float32),
            pltpu.VMEM((levels, chunks, pairs, 2 * DV, DK), jnp.float32),
            pltpu.VMEM((levels - 1, chunks, OWNED, 2 * DV, DK), jnp.float32),
            pltpu.VMEM((LANES, LANES), jnp.int32),
            dma((4, chunks)),
            dma((chunks,)),
            dma((levels, chunks)),
            dma((levels, chunks)),
            dma((levels, chunks)),
            dma((levels, chunks)),
        ],
        compiler_params=pltpu.CompilerParams(
            collective_id=0, has_side_effects=True, vmem_limit_bytes=VMEM_MIB * 1024 * 1024
        ),
    )(queries, keys, values, weights)
    return unit * out_gain


def solution(mesh):
    return jax.shard_map(
        on_device,
        mesh=mesh,
        in_specs=(
            P(("sa", "sb"), None),
            P(("sa", "sb"), None),
            P(("sa", "sb"), None),
            P(("sa", "sb"), None, None),
            P(),
        ),
        out_specs=P(("sa", "sb"), None),
        check_vma=False,
    )
```

```python
import functools

import jax
import jax.numpy as jnp
from jax import lax
from jax.experimental import pallas as pl
from jax.experimental.pallas import tpu as pltpu
from jax.sharding import PartitionSpec as P

DK = 128
DV = 64
TOK_BITS = 9
LANES = 128
TILE_BITS = 7
ROWS = 256
OWNED = 1
NEAR = 3
SIDE_GAP = 2
FIRST = 1
LAST_GAP = 1
VMEM_MIB = 56
NEAR_GAP = 2
FAR_GAP = 2

epsilon = 1e-06
MESH = pl.DeviceIdType.MESH
NT = (((1,), (1,)), ((), ()))
TN = (((0,), (0,)), ((), ()))


def lane_gather(value, index):
    return jnp.take_along_axis(value, index, axis=1, mode="promise_in_bounds")


def kernel(
    inner_bits, levels, chunks, slots, zero_slot, heads,
    q_hbm, k_hbm, v_hbm, w_hbm, out_hbm,
    qb, kb, vb, wt, wb, acc, ob, st, lvl, car, table,
    in_sem, out_sem, send_sem, recv_sem, pass_send, pass_recv, side_send, side_recv,
):
    inner, outer = lax.axis_index("sb"), lax.axis_index("sa")
    length = qb.shape[1]
    pairs = 2 * OWNED
    core = inner % 2

    def bit(j):
        if j < inner_bits:
            return (inner // (1 << j)) % 2
        return (outer // (1 << (j - inner_bits))) % 2

    def partner(j):
        if j < inner_bits:
            return {"sb": inner + (1 << j) * (1 - 2 * bit(j))}
        return {"sa": outer + (1 << (j - inner_bits)) * (1 - 2 * bit(j))}

    def fetch(which, c):
        source, target, width = (
            (k_hbm, kb, 2 * pairs * DK), (v_hbm, vb, 2 * pairs * DV), (q_hbm, qb, 2 * pairs * DK)
        )[which]
        columns = pl.ds(pl.multiple_of(c * width, width), width)
        return pltpu.make_async_copy(source.at[:, columns], target.at[c], in_sem.at[which, c])

    weights_copy = pltpu.make_async_copy(w_hbm, wt, in_sem.at[3, 0])

    def put(c):
        width = pairs * 2 * DV
        columns = pl.ds(pl.multiple_of(c * width, width), width)
        return pltpu.make_async_copy(ob.at[c], out_hbm.at[:, columns], out_sem.at[c])

    mine = pl.ds(core * OWNED, OWNED)
    top = levels - 1
    half = pl.ds(bit(1) * DV, DV)

    def exchange(j, c):
        if j == 0:
            source, target = st.at[c], lvl.at[0, c]
        elif j == top:
            source, target = car.at[j - 1, c, :, half], lvl.at[j, c, mine, half]
        else:
            source, target = car.at[j - 1, c], lvl.at[j, c, mine]
        return pltpu.make_async_remote_copy(
            src_ref=source, dst_ref=target, send_sem=send_sem.at[j, c],
            recv_sem=recv_sem.at[j, c], device_id=partner(j), device_id_type=MESH,
        )

    def across(c):
        return pltpu.make_async_remote_copy(
            src_ref=lvl.at[top, c, mine, half], dst_ref=lvl.at[top, c, mine, half], send_sem=side_send.at[c],
            recv_sem=side_recv.at[c], device_id=partner(1), device_id_type=MESH,
        )

    def pass_on(j, c):
        return pltpu.make_async_remote_copy(
            src_ref=lvl.at[j, c, mine], dst_ref=lvl.at[j, c, mine], send_sem=pass_send.at[j, c],
            recv_sem=pass_recv.at[j, c], device_id=partner(0), device_id_type=MESH,
        )

    for c in range(chunks):
        fetch(0, c).start()
        fetch(1, c).start()
        if c == 0:
            weights_copy.start()
            fetch(2, 0).start()
    for c in range(1, chunks):
        fetch(2, c).start()

    barrier = pltpu.get_barrier_semaphore()
    for j in range(levels):
        pl.semaphore_signal(barrier, inc=1, device_id=partner(j), device_id_type=MESH)

    row = lax.broadcasted_iota(jnp.int32, (LANES, LANES), 0)
    lane = lax.broadcasted_iota(jnp.int32, (LANES, LANES), 1)
    xored = jnp.bitwise_xor(row, lane)
    level = jnp.zeros((LANES, LANES), jnp.int32)
    for b in range(TILE_BITS):
        level = level + (xored >= (1 << b)).astype(jnp.int32)
    table[...] = jnp.where(row >= lane, level, zero_slot)
    pl.semaphore_wait(barrier, levels)

    def weight_place(c):
        start = c * (2 * pairs * slots)
        return start // LANES, start % LANES

    def spread_weights(group):
        shape = (wt.shape[0], LANES)
        slot = lax.broadcasted_iota(jnp.int32, shape, 1) + group * LANES
        wanted = (slot & (slots - 1)) * heads + lax.shift_right_logical(slot, slots.bit_length() - 1)
        chosen = (lax.broadcasted_iota(jnp.int32, shape, 0) == wanted).astype(jnp.bfloat16)
        wb[group] = lax.dot_general(wt[...], chosen, TN, preferred_element_type=jnp.float32)

    def block_states(c):
        for p in range(pairs):
            v = vb[c, :, p * 2 * DV : (p + 1) * 2 * DV]
            k = kb[c, :, p * 2 * DK : (p + 1) * 2 * DK]
            both = lax.dot_general(v, k, TN, preferred_element_type=jnp.float32)
            st[c, p, :DV, :] = both[:DV, :DK]
            st[c, p, DV:, :] = both[DV:, DK:]

    def local(c):
        group, offset = weight_place(c)
        for p in range(pairs):
            v = vb[c, :, p * 2 * DV : (p + 1) * 2 * DV]
            first = lax.broadcasted_iota(jnp.int32, v.shape, 1) < DV
            sides = (jnp.where(first, v, jnp.zeros_like(v)), jnp.where(first, jnp.zeros_like(v), v))
            for start in range(0, length, ROWS):
                total = None
                end = start + ROWS
                for side in range(2):
                    head = 2 * p + side
                    base = offset + head * slots
                    columns = slice(head * DK, (head + 1) * DK)
                    scores = lax.dot_general(
                        qb[c, start:end, columns], kb[c, :end, columns], NT,
                        preferred_element_type=jnp.float32,
                    )
                    strips = []
                    for t in range(start, end, LANES):
                        rows = wb[group, t : t + LANES, :]
                        strip, known = [], {}
                        for s in range(0, end, LANES):
                            if s > t:
                                strip.append(jnp.zeros((LANES, LANES), jnp.bfloat16))
                                continue
                            if s == t:
                                weight = lane_gather(rows, table[...] + base)
                            else:
                                number = (t ^ s).bit_length()
                                if number not in known:
                                    known[number] = lane_gather(
                                        rows, jnp.zeros((LANES, LANES), jnp.int32) + (base + number)
                                    )
                                weight = known[number]
                            piece = scores[t - start : t - start + LANES, s : s + LANES]
                            strip.append((piece * weight).astype(jnp.bfloat16))
                        strips.append(jnp.concatenate(strip, axis=1))
                    weighted = jnp.concatenate(strips, axis=0)
                    part = jnp.dot(weighted, sides[side][:end], preferred_element_type=jnp.float32)
                    total = part if total is None else total + part
                acc[c, start:end, p * LANES : (p + 1) * LANES] = total

    def finish(c):
        group, offset = weight_place(c)
        for p in range(pairs):
            states = []
            zero = jnp.zeros((DV, DK), jnp.bfloat16)
            for j in range(levels):
                state = jnp.where(bit(j) == 1, lvl[j, c, p], 0.0).astype(jnp.bfloat16)
                states.append(jnp.concatenate([state[:DV], zero], axis=1))
                states.append(jnp.concatenate([zero, state[DV:]], axis=1))
            for start in range(0, length, ROWS):
                q = qb[c, start : start + ROWS, p * 2 * DK : (p + 1) * 2 * DK]
                rows = wb[group, start : start + ROWS, :]
                right = (lax.broadcasted_iota(jnp.int32, (ROWS, LANES), 1) >= DV).astype(jnp.int32)
                place = right * slots + (offset + 2 * p * slots + TOK_BITS + 1)
                total = acc[c, start : start + ROWS, p * LANES : (p + 1) * LANES]
                for j in range(0, levels, 2):
                    stacked = jnp.concatenate(states[2 * j : 2 * j + 4], axis=0)
                    read = lax.dot_general(q, stacked, NT, preferred_element_type=jnp.float32)
                    for i in range(j, min(j + 2, levels)):
                        total = total + lane_gather(rows, place + i) * read[:, (i - j) * LANES : (i - j + 1) * LANES]
                square = total * total
                left = jnp.sum(jnp.where(right == 0, square, 0.0), axis=1, keepdims=True)
                other = jnp.sum(jnp.where(right == 0, 0.0, square), axis=1, keepdims=True)
                scale = jnp.where(
                    right == 0, lax.rsqrt(left * (1.0 / DV) + epsilon), lax.rsqrt(other * (1.0 / DV) + epsilon)
                )
                ob[c, start : start + ROWS, p * LANES : (p + 1) * LANES] = (total * scale).astype(jnp.bfloat16)

    arrival = [FIRST]
    for j in range(1, levels):
        arrival.append(arrival[-1] + (NEAR_GAP if j < NEAR else FAR_GAP))
    crossed = arrival[-1] + SIDE_GAP
    last = crossed + LAST_GAP

    @pl.loop(0, chunks + last)
    def _(tick):
        @pl.when(tick < chunks)
        def _():
            fetch(0, tick).wait()
            fetch(1, tick).wait()
            block_states(tick)
            exchange(0, tick).start()

        for j in range(levels):
            c = tick - arrival[j]

            @pl.when((c >= 0) & (c < chunks))
            def _(j=j, c=c):
                exchange(j, c).wait_recv()
                if j == top:
                    across(c).start()
                elif j > 0:
                    pass_on(j, c).start()
                if j + 1 < levels:
                    own = st[c, mine] if j == 0 else car[j - 1, c]
                    car[j, c] = own + lvl[j, c, mine]
                    exchange(j + 1, c).start()

        @pl.when((tick >= crossed) & (tick < crossed + chunks))
        def _():
            across(tick - crossed).wait_recv()
            pass_on(top, tick - crossed).start()

        @pl.when(tick == 0)
        def _():
            weights_copy.wait()

        @pl.when(tick < chunks)
        def _():
            fetch(2, tick).wait()
            group, offset = weight_place(tick)

            @pl.when(offset == 0)
            def _():
                spread_weights(group)

            local(tick)

        @pl.when(tick >= last)
        def _():
            c = tick - last
            for j in range(1, levels):
                pass_on(j, c).wait_recv()
            finish(c)
            put(c).start()

    @pl.loop(0, chunks)
    def _(c):
        put(c).wait()
        across(c).wait_send()
        for j in range(levels):
            exchange(j, c).wait_send()
            if j > 0:
                pass_on(j, c).wait_send()


def on_device(queries, keys, values, level_weights, out_gain):
    length = queries.shape[0]
    heads = out_gain.shape[0] // DV
    count = level_weights.shape[1]
    inner_bits = lax.axis_size("sb").bit_length() - 1
    levels = inner_bits + lax.axis_size("sa").bit_length() - 1
    slots = 1 << count.bit_length()
    pairs = 2 * OWNED
    chunks = heads // (2 * pairs)
    weights = jnp.transpose(level_weights, (1, 2, 0)).reshape(count * heads, length)
    hbm = pl.BlockSpec(memory_space=pltpu.HBM)
    dma = pltpu.SemaphoreType.DMA
    unit = pl.pallas_call(
        functools.partial(kernel, inner_bits, levels, chunks, slots, count, heads),
        out_shape=jax.ShapeDtypeStruct(values.shape, jnp.bfloat16),
        in_specs=[hbm, hbm, hbm, hbm],
        out_specs=pl.BlockSpec(memory_space=pl.ANY),
        scratch_shapes=[
            pltpu.VMEM((chunks, length, 2 * pairs * DK), jnp.bfloat16),
            pltpu.VMEM((chunks, length, 2 * pairs * DK), jnp.bfloat16),
            pltpu.VMEM((chunks, length, 2 * pairs * DV), jnp.bfloat16),
            pltpu.VMEM(weights.shape, jnp.bfloat16),
            pltpu.VMEM((heads * slots // LANES, length, LANES), jnp.float32),
            pltpu.VMEM((chunks, length, 2 * pairs * DV), jnp.float32),
            pltpu.VMEM((chunks, length, 2 * pairs * DV), jnp.bfloat16),
            pltpu.VMEM((chunks, pairs, 2 * DV, DK), jnp.float32),
            pltpu.VMEM((levels, chunks, pairs, 2 * DV, DK), jnp.float32),
            pltpu.VMEM((levels - 1, chunks, OWNED, 2 * DV, DK), jnp.float32),
            pltpu.VMEM((LANES, LANES), jnp.int32),
            dma((4, chunks)),
            dma((chunks,)),
            dma((levels, chunks)),
            dma((levels, chunks)),
            dma((levels, chunks)),
            dma((levels, chunks)),
            dma((chunks,)),
            dma((chunks,)),
        ],
        compiler_params=pltpu.CompilerParams(
            collective_id=0, has_side_effects=True, vmem_limit_bytes=VMEM_MIB * 1024 * 1024
        ),
    )(queries, keys, values, weights)
    return unit * out_gain


def solution(mesh):
    return jax.shard_map(
        on_device,
        mesh=mesh,
        in_specs=(
            P(("sa", "sb"), None),
            P(("sa", "sb"), None),
            P(("sa", "sb"), None),
            P(("sa", "sb"), None, None),
            P(),
        ),
        out_specs=P(("sa", "sb"), None),
        check_vma=False,
    )
```
